256 devices in a mesh: chan: 128 (over x_lo, z, y, core), win: 2 (over x_hi).
Axes of the slice: x: 4 (x_hi: 2, x_lo: 2; x = x_hi * 2 + x_lo), y: 4, z: 8, core: 2. Of those that a mesh axis runs over, the one named last changes fastest.
Arguments:
- spectra: bfloat16 [8, 4096, 1024], P('win', 'chan'), may hold values from -6 to 6
- source_pool: bfloat16 [8, 32768, 1024], P('win', 'chan'), may hold values from -6 to 6
- owners: int32 [4], replicated, may hold values from 0 to 127, as said below
- source_rows: int32 [4, 128], replicated, may hold values from 0 to 255, as said below
Outputs:
- stack: bfloat16 [4096, 64, 512], P('chan', None, 'win')
The draws below stay inside these ranges and needn't reach their ends.
Inputs may be any that keep to these rules, and one draw needn't show every extreme that they name: The owners are distinct; 0 and 127 are always among them. `source_rows`: within a block the rows are distinct; 0 and 255 are always among them.
All inputs are finite; a program needn't handle non-finite values.
Results may differ from the reference program's by a relative error of at most 0.0049.
Values may be sent and summed in bfloat16 or wider, within the bound.
A program may use at most 128 MiB of HBM per device.

```python
import jax
import jax.numpy as jnp
from jax import lax

BINS = 512
LAGS = 64
SB = 128
NSB = 4
POOL = 256
CH_DEV = 32
WINDOWS = 8
CHANNELS = 4096
NSRC = 512
N_CHAN = 128


def pick_distinct(key, total, count):
    middle = jax.random.permutation(key, total - 2)[:count - 2] + 1
    values = jnp.concatenate([jnp.array([0, total - 1], dtype=jnp.int32), middle.astype(jnp.int32)])
    order = jax.random.permutation(jax.random.fold_in(key, 7), count)
    return values[order].astype(jnp.int32)


def draw_owners(key, part):
    return pick_distinct(jax.random.fold_in(key, 11), CHANNELS // CH_DEV, NSB)


def draw_source_rows(key, part):
    keys = jax.random.split(jax.random.fold_in(key, 13), NSB)
    return jax.vmap(lambda single: pick_distinct(single, POOL, SB))(keys)


def block_scale(key, dims, shards, low, largest):
    factor_of = 1.0
    for axis_at, blocks in shards:
        heights = jax.random.uniform(jax.random.fold_in(jax.random.fold_in(key, 6), axis_at), (blocks,), jnp.float32, low / len(shards), largest / len(shards))
        factor_of = factor_of * jnp.repeat(jnp.exp(heights), dims[axis_at] // blocks).reshape((-1,) + (1,) * (len(dims) - 1 - axis_at))
    return factor_of


def scatter_about(key, dims, scale, most, cuts=(), held_as=jnp.bfloat16):
    values = jax.random.normal(key, dims, jnp.float32) * scale
    if len(cuts) > 0:
        values = block_scale(key, dims, cuts, -0.22, 0.18) * values
    return jnp.clip(values, min=-most, max=most).astype(held_as)


def setup_inputs(seed: int = 0) -> dict:
    key_of = jax.random.split(jax.random.key(seed), 5)
    spectra = scatter_about(key_of[0], (WINDOWS, CHANNELS, 2 * BINS), 1.0, 6.0, ((0, 2), (1, 128)))
    source_pool = scatter_about(key_of[1], (WINDOWS, N_CHAN * POOL, 2 * BINS), 1.0, 6.0, ((0, 2), (1, 128)))
    owners = draw_owners(jax.random.fold_in(key_of[4], 71), 0)
    source_rows = draw_source_rows(jax.random.fold_in(key_of[4], 71), 0)
    return dict(spectra=spectra, source_pool=source_pool, owners=owners, source_rows=source_rows)


def phase_tables():
    freq = jnp.arange(BINS, dtype=jnp.float32)
    shift = (jnp.arange(LAGS, dtype=jnp.int32) - LAGS // 2).astype(jnp.float32)
    phase = jnp.pi * shift[:, None] * freq[None, :] / BINS
    return jnp.cos(phase), jnp.sin(phase)


def modulate(spec, cosine, sine):
    values = spec.astype(jnp.float32)
    real_part = values[..., :BINS][..., None, :]
    imag_part = values[..., BINS:][..., None, :]
    scale = (2.0 * BINS) ** -0.5
    first = (real_part * cosine - imag_part * sine) * scale
    second = (imag_part * cosine + real_part * sine) * scale
    return jnp.concatenate([first, second], axis=-1).astype(jnp.bfloat16)


def reference(spectra, source_pool, owners, source_rows):
    cosine, sine = phase_tables()
    index = (owners[:, None] * POOL + source_rows).reshape(-1).astype(jnp.int32)
    source = jnp.take(source_pool, index, axis=1).astype(jnp.float32)
    blocks = spectra.reshape(WINDOWS, CHANNELS // CH_DEV, CH_DEV, 2 * BINS).transpose(1, 0, 2, 3)

    def one_block(block):
        lagged = modulate(block, cosine, sine).astype(jnp.float32)
        return jnp.einsum("wclk,wsk->cls", lagged, source).astype(jnp.bfloat16)

    stacked = lax.map(one_block, blocks)
    return stacked.reshape(CHANNELS, LAGS, NSRC)
```

```python
import functools

import jax
import jax.numpy as jnp
import numpy as np
from jax import lax
from jax.experimental import pallas as pl
from jax.experimental.pallas import tpu as pltpu
from jax.sharding import PartitionSpec as P

LAGS = 64
BINS = 512
LANES = 128
MESH = pl.DeviceIdType.MESH
NX, NZ, NY, NC, NH = 2, 8, 4, 2, 2
PLANE = NX * NY * NC
COLUMN = NH * NZ
WAVES = 2


def phase_tables():
    freq = np.arange(BINS, dtype=np.float64)
    shift = np.arange(LAGS, dtype=np.float64) - LAGS // 2
    phase = np.pi * shift[:, None] * freq[None, :] / BINS
    scale = (2.0 * BINS) ** -0.5
    return (
        (np.cos(phase) * scale).astype(np.float32),
        (np.sin(phase) * scale).astype(np.float32),
    )


def kernel(
    owners, rows_ref, cos_ref, sin_ref, spec_ref, pool_hbm, out_ref,
    pool, mine, cand_a, cand_b, slots, cand2_a, cand2_b, red, pieces, spec_in, spec32, mod, acc,
    pool_sem, rs1_send, rs1_recv, rs2_send, rs2_recv, ag1_send, ag1_recv,
    ring_send, ring_recv, sib_send, sib_recv, spec_send, spec_recv,
):
    chan = lax.axis_index("chan")
    half = lax.axis_index("win")
    x, z = chan // 64, (chan // 8) % 8
    y, core = (chan // 2) % 4, chan % 2
    q = x * NY + y
    s = q * NC + core
    t = half * NZ + z

    def device(x, y, z, core, half):
        return (x * 64 + z * 8 + y * 2 + core, half)

    def plane_device(index):
        return device(index // 8, (index // 2) % 4, z, index % 2, half)

    def column_device(index):
        return device(x, y, index % NZ, core, index // NZ)

    def piece(v, zz, cc):
        return (v * NZ + zz) * NC + cc

    up = device(x, y, (z + 1) % NZ, core, half)
    down = device(x, y, (z + NZ - 1) % NZ, core, half)
    sibling = device(x, y, z, 1 - core, half)
    partner = device(x, y, z, core, 1 - half)

    loads = []
    for w in range(4):
        load = pltpu.make_async_copy(pool_hbm.at[w], pool.at[w], pool_sem.at[w])
        load.start()
        loads.append(load)

    barrier = pltpu.get_barrier_semaphore()
    for j in range(1, PLANE):
        pl.semaphore_signal(
            barrier, inc=1, device_id=plane_device((s + j) % PLANE), device_id_type=MESH
        )
    for j in range(1, COLUMN):
        pl.semaphore_signal(
            barrier, inc=1, device_id=column_device((t + j) % COLUMN), device_id_type=MESH
        )

    target = jnp.full((128, 1), -1, jnp.int32)
    for b in range(4):
        target = jnp.where(owners[b] == chan, rows_ref[:, b : b + 1], target)
    onehot = (lax.broadcasted_iota(jnp.int32, (128, 256), 1) == target).astype(jnp.float32)
    onehot = onehot.astype(jnp.bfloat16)
    for w in range(4):
        loads[w].wait()
        picked = jnp.dot(onehot, pool[w], preferred_element_type=jnp.float32)
        picked = picked.astype(jnp.bfloat16)
        for group in range(8):
            kh, cc, v = group // 4, (group // 2) % 2, group % 2
            for qq in range(8):
                mine[v, qq * NC + cc, 2 * w + kh] = picked[
                    qq * 16 : qq * 16 + 16, group * LANES : (group + 1) * LANES
                ]

    pl.semaphore_wait(barrier, PLANE + COLUMN - 2)

    sends = []
    cand, cand2 = (cand_a, cand_b), (cand2_a, cand2_b)

    def remote(src, dst, send_sem, recv_sem, where):
        copy = pltpu.make_async_remote_copy(
            src_ref=src, dst_ref=dst, send_sem=send_sem, recv_sem=recv_sem,
            device_id=where, device_id_type=MESH,
        )
        return copy

    def send(*args):
        copy = remote(*args)
        copy.start()
        sends.append(copy)

    def wait_recv(ref, recv_sem):
        remote(ref, ref, recv_sem, recv_sem, sibling).wait_recv()

    for v in range(WAVES):
        for j in range(1, PLANE):
            to = (s + j) % PLANE
            send(mine.at[v, to], cand[v].at[s], rs1_send.at[v, j], rs1_recv.at[v, s], plane_device(to))
        cand[v][s] = mine[v, s]
    send(spec_ref, spec_in, spec_send, spec_recv, partner)

    def modulate(hh):
        def body(i, carry):
            w, r = i // 8, (i % 8) * 4
            for g in range(4):
                cosine = cos_ref[:, g * LANES : (g + 1) * LANES]
                sine = sin_ref[:, g * LANES : (g + 1) * LANES]
                for k in range(4):
                    row = pl.ds(r + k, 8, stride=0)
                    a = jnp.tile(spec32[w, g, row, :], (8, 1))
                    b = jnp.tile(spec32[w, 4 + g, row, :], (8, 1))
                    first = (a * cosine - b * sine).astype(jnp.bfloat16)
                    second = (b * cosine + a * sine).astype(jnp.bfloat16)
                    at = pl.ds(pl.multiple_of((r + k) * LAGS, LAGS), LAGS)
                    mod[piece(g % 2, 2 * w, g // 2), hh, at, :] = first
                    mod[piece(g % 2, 2 * w + 1, g // 2), hh, at, :] = second
            return carry

        lax.fori_loop(0, 32, body, 0)

    def widen(ref):
        for g in range(8):
            spec32[:, g] = ref[:, :, g * LANES : (g + 1) * LANES].astype(jnp.float32)

    widen(spec_ref)
    modulate(half)

    for v in range(WAVES):
        for j in range(1, PLANE):
            frm = (s + j) % PLANE
            wait_recv(cand[v].at[frm], rs1_recv.at[v, frm])
        for b in range(4):
            at = (owners[b] // 64) * 8 + owners[b] % 8
            slots[v, b // 2, :, b % 2] = cand[v][at]
        for j in range(1, COLUMN):
            to = (t + j) % COLUMN
            send(slots.at[v, to // NZ, to % NZ], cand2[v].at[half, z], rs2_send.at[v, j], rs2_recv.at[v, t], column_device(to))
        cand2[v][half, z] = slots[v, half, z]

    wait_recv(spec_in, spec_recv)
    widen(spec_in)
    modulate(1 - half)

    for v in range(WAVES):
        for j in range(1, COLUMN):
            frm = (t + j) % COLUMN
            wait_recv(cand2[v].at[frm // NZ, frm % NZ], rs2_recv.at[v, frm])
        for hh in range(NH):
            for bb in range(2):
                zz = (owners[2 * half + bb] // 8) % 8
                red[v, 2 * hh + bb] = cand2[v][hh, zz, bb]
        for j in range(1, NX * NY):
            to = (q + j) % (NX * NY)
            p = piece(v, z, core)
            send(red.at[v], pieces.at[p, :, q], ag1_send.at[v, j], ag1_recv.at[v, q], device(to // 4, to % 4, z, core, half))
        pieces[piece(v, z, core), :, q] = red[v]

    def multiply(indices, start):
        total = len(indices)

        def body(i, carry):
            at = pl.ds(pl.multiple_of(i * 1024, 1024), 1024)
            result = None
            for p in indices:
                left = jnp.concatenate([mod[p, 0, at, :], mod[p, 1, at, :]], axis=1)
                right = jnp.concatenate(
                    [pieces[p, 0:2].reshape(256, LANES), pieces[p, 2:4].reshape(256, LANES)], axis=1
                )
                term = lax.dot_general(
                    left, right, (((1,), (1,)), ((), ())), preferred_element_type=jnp.float32
                )
                result = term if result is None else result + term
            if not start:
                result = result + acc[at, :]
            acc[at, :] = result
            return carry

        lax.fori_loop(0, 2, body, 0)

    def forward(v, zz):
        p = piece(v, zz, core)
        send(pieces.at[p], pieces.at[p], sib_send.at[v, zz], sib_recv.at[v, zz], sibling)

    for v in range(WAVES):
        p = piece(v, z, core)
        for j in range(1, NX * NY):
            frm = (q + j) % (NX * NY)
            wait_recv(pieces.at[p, :, frm], ag1_recv.at[v, frm])
        send(pieces.at[p], pieces.at[p], ring_send.at[v, 0, 0], ring_recv.at[v, 0, 0], up)
        send(pieces.at[p], pieces.at[p], ring_send.at[v, 0, 1], ring_recv.at[v, 0, 1], down)
        forward(v, z)

    multiply([piece(0, z, core), piece(1, z, core)], True)

    def sibling_ready(v, zz):
        p = piece(v, zz, 1 - core)
        wait_recv(pieces.at[p], sib_recv.at[v, zz])

    ready = [z]
    for d in range(1, 5):
        below, above = (z + NZ - d) % NZ, (z + d) % NZ
        for v in range(WAVES):
            pb, pa = piece(v, below, core), piece(v, above, core)
            if d < 4:
                wait_recv(pieces.at[pb], ring_recv.at[v, d - 1, 0])
                if d < 3:
                    send(pieces.at[pb], pieces.at[pb], ring_send.at[v, d, 0], ring_recv.at[v, d, 0], up)
                else:
                    part = pieces.at[pb, 0:2]
                    send(part, part, ring_send.at[v, d, 0], ring_recv.at[v, d, 0], up)
                forward(v, below)
                wait_recv(pieces.at[pa], ring_recv.at[v, d - 1, 1])
                if d < 3:
                    send(pieces.at[pa], pieces.at[pa], ring_send.at[v, d, 1], ring_recv.at[v, d, 1], down)
                else:
                    part = pieces.at[pa, 2:4]
                    send(part, part, ring_send.at[v, d, 1], ring_recv.at[v, d, 1], down)
                forward(v, above)
            else:
                wait_recv(pieces.at[pb, 0:2], ring_recv.at[v, d - 1, 0])
                wait_recv(pieces.at[pa, 2:4], ring_recv.at[v, d - 1, 1])
                forward(v, below)
        for zz in ready:
            for v in range(WAVES):
                sibling_ready(v, zz)
            multiply([piece(0, zz, 1 - core), piece(1, zz, 1 - core)], False)
        ready = [below, above] if d < 4 else [below]
        for zz in ready:
            multiply([piece(0, zz, core), piece(1, zz, core)], False)
    for zz in ready:
        for v in range(WAVES):
            sibling_ready(v, zz)
        multiply([piece(0, zz, 1 - core), piece(1, zz, 1 - core)], False)

    out_ref[...] = acc[...].astype(jnp.bfloat16)
    for copy in sends:
        copy.wait_send()


def on_device(spectra, source_pool, owners, source_rows):
    cosine, sine = phase_tables()
    vmem = pl.BlockSpec(memory_space=pltpu.VMEM)
    dma = pltpu.SemaphoreType.DMA
    b16 = jnp.bfloat16
    out = pl.pallas_call(
        kernel,
        out_shape=jax.ShapeDtypeStruct((32 * LAGS, 256), b16),
        in_specs=[pl.BlockSpec(memory_space=pltpu.SMEM), vmem, vmem, vmem, vmem, pl.BlockSpec(memory_space=pl.ANY)],
        out_specs=vmem,
        scratch_shapes=[
            pltpu.VMEM((4, 256, 1024), b16),
            pltpu.VMEM((WAVES, PLANE, 8, 16, LANES), b16),
            pltpu.VMEM((PLANE, 8, 16, LANES), b16),
            pltpu.VMEM((PLANE, 8, 16, LANES), b16),
            pltpu.VMEM((WAVES, NH, NZ, 2, 16, LANES), b16),
            pltpu.VMEM((NH, NZ, 2, 16, LANES), b16),
            pltpu.VMEM((NH, NZ, 2, 16, LANES), b16),
            pltpu.VMEM((WAVES, 4, 16, LANES), b16),
            pltpu.VMEM((WAVES * NZ * NC, 4, 8, 16, LANES), b16),
            pltpu.VMEM((4, 32, 1024), b16),
            pltpu.VMEM((4, 8, 32, LANES), jnp.float32),
            pltpu.VMEM((WAVES * NZ * NC, NH, 32 * LAGS, LANES), b16),
            pltpu.VMEM((32 * LAGS, 256), jnp.float32),
            dma((4,)),
            dma((WAVES, PLANE)),
            dma((WAVES, PLANE)),
            dma((WAVES, COLUMN)),
            dma((WAVES, COLUMN)),
            dma((WAVES, 8)),
            dma((WAVES, 8)),
            dma((WAVES, 4, 2)),
            dma((WAVES, 4, 2)),
            dma((WAVES, NZ)),
            dma((WAVES, NZ)),
            dma,
            dma,
        ],
        compiler_params=pltpu.CompilerParams(
            collective_id=0, has_side_effects=True, vmem_limit_bytes=62 * 2**20
        ),
    )(owners, source_rows.T, jnp.asarray(cosine), jnp.asarray(sine), spectra, source_pool)
    return out.reshape(32, LAGS, 256)


def solution(mesh):
    placed = (P("win", "chan", None), P("win", "chan", None), P(), P())
    return jax.shard_map(
        on_device, mesh=mesh, in_specs=placed, out_specs=P("chan", None, "win"), check_vma=False
    )
```

```python
import functools

import jax
import jax.numpy as jnp
import numpy as np
from jax import lax
from jax.experimental import pallas as pl
from jax.experimental.pallas import tpu as pltpu
from jax.sharding import PartitionSpec as P

LAGS = 64
BINS = 512
LANES = 128
MESH = pl.DeviceIdType.MESH
NX, NZ, NY, NC, NH = 2, 8, 4, 2, 2
PLANE = NX * NY * NC
COLUMN = NH * NZ
WAVES = 2
ROWS = 512


def phase_tables():
    freq = np.arange(BINS, dtype=np.float64)
    shift = np.arange(LAGS, dtype=np.float64) - LAGS // 2
    phase = np.pi * shift[:, None] * freq[None, :] / BINS
    scale = (2.0 * BINS) ** -0.5
    return (
        (np.cos(phase) * scale).astype(np.float32),
        (np.sin(phase) * scale).astype(np.float32),
    )


def kernel(
    owners, rows_ref, cos_ref, sin_ref, spec_ref, pool_hbm, out_ref,
    pool, mine, cand_a, cand_b, slots, cand2_a, cand2_b, red, pieces, spec_in, spec32, mod, acc,
    pool_sem, rs1_send, rs1_recv, rs2_send, rs2_recv, ag1_send, ag1_recv,
    ring_send, ring_recv, sib_send, sib_recv, spec_send, spec_recv,
):
    chan = lax.axis_index("chan")
    half = lax.axis_index("win")
    x, z = chan // 64, (chan // 8) % 8
    y, core = (chan // 2) % 4, chan % 2
    q = x * NY + y
    s = q * NC + core
    t = half * NZ + z

    def device(x, y, z, core, half):
        return (x * 64 + z * 8 + y * 2 + core, half)

    def plane_device(index):
        return device(index // 8, (index // 2) % 4, z, index % 2, half)

    def column_device(index):
        return device(x, y, index % NZ, core, index // NZ)

    def piece(v, zz, cc):
        return (v * NZ + zz) * NC + cc

    up = device(x, y, (z + 1) % NZ, core, half)
    down = device(x, y, (z + NZ - 1) % NZ, core, half)
    sibling = device(x, y, z, 1 - core, half)
    partner = device(x, y, z, core, 1 - half)

    loads = []
    for w in range(4):
        load = pltpu.make_async_copy(pool_hbm.at[w], pool.at[w], pool_sem.at[w])
        load.start()
        loads.append(load)

    barrier = pltpu.get_barrier_semaphore()
    for j in range(1, PLANE):
        pl.semaphore_signal(
            barrier, inc=1, device_id=plane_device((s + j) % PLANE), device_id_type=MESH
        )
    for j in range(1, COLUMN):
        pl.semaphore_signal(
            barrier, inc=1, device_id=column_device((t + j) % COLUMN), device_id_type=MESH
        )

    target = jnp.full((128, 1), -1, jnp.int32)
    for b in range(4):
        target = jnp.where(owners[b] == chan, rows_ref[:, b : b + 1], target)
    onehot = (lax.broadcasted_iota(jnp.int32, (128, 256), 1) == target).astype(jnp.float32)
    onehot = onehot.astype(jnp.bfloat16)
    for w in range(4):
        loads[w].wait()
        picked = jnp.dot(onehot, pool[w], preferred_element_type=jnp.float32)
        picked = picked.astype(jnp.bfloat16)
        for group in range(8):
            kh, cc, v = group // 4, (group // 2) % 2, group % 2
            for qq in range(8):
                mine[v, qq * NC + cc, 2 * w + kh] = picked[
                    qq * 16 : qq * 16 + 16, group * LANES : (group + 1) * LANES
                ]

    pl.semaphore_wait(barrier, PLANE + COLUMN - 2)

    sends = []
    cand, cand2 = (cand_a, cand_b), (cand2_a, cand2_b)

    def remote(src, dst, send_sem, recv_sem, where):
        copy = pltpu.make_async_remote_copy(
            src_ref=src, dst_ref=dst, send_sem=send_sem, recv_sem=recv_sem,
            device_id=where, device_id_type=MESH,
        )
        return copy

    def send(*args):
        copy = remote(*args)
        copy.start()
        sends.append(copy)

    def wait_recv(ref, recv_sem):
        remote(ref, ref, recv_sem, recv_sem, sibling).wait_recv()

    for v in range(WAVES):
        for j in range(1, PLANE):
            to = (s + j) % PLANE
            send(mine.at[v, to], cand[v].at[s], rs1_send.at[v, j], rs1_recv.at[v, s], plane_device(to))
        cand[v][s] = mine[v, s]
    send(spec_ref, spec_in, spec_send, spec_recv, partner)

    def modulate(hh, first_window, last_window):
        def body(i, carry):
            w, r = i // 8, (i % 8) * 4
            for g in range(4):
                cosine = cos_ref[:, g * LANES : (g + 1) * LANES]
                sine = sin_ref[:, g * LANES : (g + 1) * LANES]
                for k in range(4):
                    row = pl.ds(r + k, 8, stride=0)
                    a = jnp.tile(spec32[w, g, row, :], (8, 1))
                    b = jnp.tile(spec32[w, 4 + g, row, :], (8, 1))
                    first = (a * cosine - b * sine).astype(jnp.bfloat16)
                    second = (b * cosine + a * sine).astype(jnp.bfloat16)
                    at = pl.ds(pl.multiple_of((r + k) * LAGS, LAGS), LAGS)
                    mod[piece(g % 2, 2 * w, g // 2), hh, at, :] = first
                    mod[piece(g % 2, 2 * w + 1, g // 2), hh, at, :] = second
            return carry

        lax.fori_loop(8 * first_window, 8 * last_window, body, 0)

    def widen(ref):
        for g in range(8):
            spec32[:, g] = ref[:, :, g * LANES : (g + 1) * LANES].astype(jnp.float32)

    widen(spec_ref)
    modulate(half, 0, 4)

    for v in range(WAVES):
        for j in range(1, PLANE):
            frm = (s + j) % PLANE
            wait_recv(cand[v].at[frm], rs1_recv.at[v, frm])
        for b in range(4):
            at = (owners[b] // 64) * 8 + owners[b] % 8
            slots[v, b // 2, :, b % 2] = cand[v][at]
        for j in range(1, COLUMN):
            to = (t + j) % COLUMN
            send(slots.at[v, to // NZ, to % NZ], cand2[v].at[half, z], rs2_send.at[v, j], rs2_recv.at[v, t], column_device(to))
        cand2[v][half, z] = slots[v, half, z]

    wait_recv(spec_in, spec_recv)
    widen(spec_in)
    modulate(1 - half, 0, 2)

    for v in range(WAVES):
        for j in range(1, COLUMN):
            frm = (t + j) % COLUMN
            wait_recv(cand2[v].at[frm // NZ, frm % NZ], rs2_recv.at[v, frm])
        for hh in range(NH):
            for bb in range(2):
                zz = (owners[2 * half + bb] // 8) % 8
                red[v, 2 * hh + bb] = cand2[v][hh, zz, bb]
        for j in range(1, NX * NY):
            to = (q + j) % (NX * NY)
            p = piece(v, z, core)
            send(red.at[v], pieces.at[p, :, q], ag1_send.at[v, j], ag1_recv.at[v, q], device(to // 4, to % 4, z, core, half))
        pieces[piece(v, z, core), :, q] = red[v]

    modulate(1 - half, 2, 3)

    def multiply(indices, start):
        def body(i, carry):
            at = pl.ds(pl.multiple_of(i * ROWS, ROWS), ROWS)
            left = jnp.concatenate([mod[p, hh, at, :] for p in indices for hh in range(NH)], axis=1)
            right = jnp.concatenate(
                [
                    pieces[p, 2 * hh : 2 * hh + 2].reshape(256, LANES)
                    for p in indices
                    for hh in range(NH)
                ],
                axis=1,
            )
            result = lax.dot_general(
                left, right, (((1,), (1,)), ((), ())), preferred_element_type=jnp.float32
            )
            if not start:
                result = result + acc[at, :]
            acc[at, :] = result
            return carry

        lax.fori_loop(0, 32 * LAGS // ROWS, body, 0)

    def forward(v, zz):
        p = piece(v, zz, core)
        send(pieces.at[p], pieces.at[p], sib_send.at[v, zz], sib_recv.at[v, zz], sibling)

    for v in range(WAVES):
        p = piece(v, z, core)
        for j in range(1, NX * NY):
            frm = (q + j) % (NX * NY)
            wait_recv(pieces.at[p, :, frm], ag1_recv.at[v, frm])
        send(pieces.at[p], pieces.at[p], ring_send.at[v, 0, 0], ring_recv.at[v, 0, 0], up)
        send(pieces.at[p], pieces.at[p], ring_send.at[v, 0, 1], ring_recv.at[v, 0, 1], down)
        forward(v, z)

    modulate(1 - half, 3, 4)
    multiply([piece(0, z, core), piece(1, z, core)], True)

    def sibling_ready(v, zz):
        p = piece(v, zz, 1 - core)
        wait_recv(pieces.at[p], sib_recv.at[v, zz])

    ready = [z]
    for d in range(1, 5):
        below, above = (z + NZ - d) % NZ, (z + d) % NZ
        for v in range(WAVES):
            pb, pa = piece(v, below, core), piece(v, above, core)
            if d < 4:
                wait_recv(pieces.at[pb], ring_recv.at[v, d - 1, 0])
                if d < 3:
                    send(pieces.at[pb], pieces.at[pb], ring_send.at[v, d, 0], ring_recv.at[v, d, 0], up)
                else:
                    part = pieces.at[pb, 0:2]
                    send(part, part, ring_send.at[v, d, 0], ring_recv.at[v, d, 0], up)
                forward(v, below)
                wait_recv(pieces.at[pa], ring_recv.at[v, d - 1, 1])
                if d < 3:
                    send(pieces.at[pa], pieces.at[pa], ring_send.at[v, d, 1], ring_recv.at[v, d, 1], down)
                else:
                    part = pieces.at[pa, 2:4]
                    send(part, part, ring_send.at[v, d, 1], ring_recv.at[v, d, 1], down)
                forward(v, above)
            else:
                wait_recv(pieces.at[pb, 0:2], ring_recv.at[v, d - 1, 0])
                wait_recv(pieces.at[pa, 2:4], ring_recv.at[v, d - 1, 1])
                forward(v, below)
        for zz in ready:
            for v in range(WAVES):
                sibling_ready(v, zz)
        indices = [piece(v, zz, 1 - core) for zz in ready for v in range(WAVES)]
        ready = [below, above] if d < 4 else [below]
        indices += [piece(v, zz, core) for zz in ready for v in range(WAVES)]
        multiply(indices, False)
    for zz in ready:
        for v in range(WAVES):
            sibling_ready(v, zz)
        multiply([piece(0, zz, 1 - core), piece(1, zz, 1 - core)], False)

    out_ref[...] = acc[...].astype(jnp.bfloat16)
    for copy in sends:
        copy.wait_send()


def on_device(spectra, source_pool, owners, source_rows):
    cosine, sine = phase_tables()
    vmem = pl.BlockSpec(memory_space=pltpu.VMEM)
    dma = pltpu.SemaphoreType.DMA
    b16 = jnp.bfloat16
    out = pl.pallas_call(
        kernel,
        out_shape=jax.ShapeDtypeStruct((32 * LAGS, 256), b16),
        in_specs=[pl.BlockSpec(memory_space=pltpu.SMEM), vmem, vmem, vmem, vmem, pl.BlockSpec(memory_space=pl.ANY)],
        out_specs=vmem,
        scratch_shapes=[
            pltpu.VMEM((4, 256, 1024), b16),
            pltpu.VMEM((WAVES, PLANE, 8, 16, LANES), b16),
            pltpu.VMEM((PLANE, 8, 16, LANES), b16),
            pltpu.VMEM((PLANE, 8, 16, LANES), b16),
            pltpu.VMEM((WAVES, NH, NZ, 2, 16, LANES), b16),
            pltpu.VMEM((NH, NZ, 2, 16, LANES), b16),
            pltpu.VMEM((NH, NZ, 2, 16, LANES), b16),
            pltpu.VMEM((WAVES, 4, 16, LANES), b16),
            pltpu.VMEM((WAVES * NZ * NC, 4, 8, 16, LANES), b16),
            pltpu.VMEM((4, 32, 1024), b16),
            pltpu.VMEM((4, 8, 32, LANES), jnp.float32),
            pltpu.VMEM((WAVES * NZ * NC, NH, 32 * LAGS, LANES), b16),
            pltpu.VMEM((32 * LAGS, 256), jnp.float32),
            dma((4,)),
            dma((WAVES, PLANE)),
            dma((WAVES, PLANE)),
            dma((WAVES, COLUMN)),
            dma((WAVES, COLUMN)),
            dma((WAVES, 8)),
            dma((WAVES, 8)),
            dma((WAVES, 4, 2)),
            dma((WAVES, 4, 2)),
            dma((WAVES, NZ)),
            dma((WAVES, NZ)),
            dma,
            dma,
        ],
        compiler_params=pltpu.CompilerParams(
            collective_id=0, has_side_effects=True, vmem_limit_bytes=62 * 2**20
        ),
    )(owners, source_rows.T, jnp.asarray(cosine), jnp.asarray(sine), spectra, source_pool)
    return out.reshape(32, LAGS, 256)


def solution(mesh):
    placed = (P("win", "chan", None), P("win", "chan", None), P(), P())
    return jax.shard_map(
        on_device, mesh=mesh, in_specs=placed, out_specs=P("chan", None, "win"), check_vma=False
    )
```

```python
import functools

import jax
import jax.numpy as jnp
import numpy as np
from jax import lax
from jax.experimental import pallas as pl
from jax.experimental.pallas import tpu as pltpu
from jax.sharding import PartitionSpec as P

LAGS = 64
BINS = 512
LANES = 128
MESH = pl.DeviceIdType.MESH
NX, NZ, NY, NC, NH = 2, 8, 4, 2, 2
PLANE = NX * NY * NC
COLUMN = NH * NZ
WAVES = 2
ROWS = 512


def phase_tables():
    freq = np.arange(BINS, dtype=np.float64)
    shift = np.arange(LAGS, dtype=np.float64) - LAGS // 2
    phase = np.pi * shift[:, None] * freq[None, :] / BINS
    scale = (2.0 * BINS) ** -0.5
    return (
        (np.cos(phase) * scale).astype(np.float32),
        (np.sin(phase) * scale).astype(np.float32),
    )


def kernel(
    owners, rows_ref, cos_ref, sin_ref, spec_ref, pool_hbm, out_ref,
    pool, mine, cand_a, cand_b, slots, cand2_a, cand2_b, red, pieces, spec_in, spec32, mod, acc,
    pool_sem, rs1_send, rs1_recv, rs2_send, rs2_recv, ag1_send, ag1_recv,
    agz_send, agz_recv, agxy_send, agxy_recv,
    ring_send, ring_recv, sib_send, sib_recv, spec_send, spec_recv,
):
    chan = lax.axis_index("chan")
    half = lax.axis_index("win")
    x, z = chan // 64, (chan // 8) % 8
    y, core = (chan // 2) % 4, chan % 2
    q = x * NY + y
    s = q * NC + core
    t = half * NZ + z

    def device(x, y, z, core, half):
        return (x * 64 + z * 8 + y * 2 + core, half)

    def plane_device(index):
        return device(index // 8, (index // 2) % 4, z, index % 2, half)

    def column_device(index):
        return device(x, y, index % NZ, core, index // NZ)

    def piece(v, zz, cc):
        return (v * NZ + zz) * NC + cc

    up = device(x, y, (z + 1) % NZ, core, half)
    down = device(x, y, (z + NZ - 1) % NZ, core, half)
    sibling = device(x, y, z, 1 - core, half)
    partner = device(x, y, z, core, 1 - half)

    loads = []
    for w in range(4):
        load = pltpu.make_async_copy(pool_hbm.at[w], pool.at[w], pool_sem.at[w])
        load.start()
        loads.append(load)

    barrier = pltpu.get_barrier_semaphore()
    for j in range(1, PLANE):
        pl.semaphore_signal(
            barrier, inc=1, device_id=plane_device((s + j) % PLANE), device_id_type=MESH
        )
    for j in range(1, COLUMN):
        pl.semaphore_signal(
            barrier, inc=1, device_id=column_device((t + j) % COLUMN), device_id_type=MESH
        )

    target = jnp.full((128, 1), -1, jnp.int32)
    for b in range(4):
        target = jnp.where(owners[b] == chan, rows_ref[:, b : b + 1], target)
    onehot = (lax.broadcasted_iota(jnp.int32, (128, 256), 1) == target).astype(jnp.float32)
    onehot = onehot.astype(jnp.bfloat16)
    for w in range(4):
        loads[w].wait()
        picked = jnp.dot(onehot, pool[w], preferred_element_type=jnp.float32)
        picked = picked.astype(jnp.bfloat16)
        for group in range(8):
            kh, cc, v = group // 4, (group // 2) % 2, group % 2
            for qq in range(8):
                mine[v, qq * NC + cc, 2 * w + kh] = picked[
                    qq * 16 : qq * 16 + 16, group * LANES : (group + 1) * LANES
                ]

    pl.semaphore_wait(barrier, PLANE + COLUMN - 2)

    sends = []
    cand, cand2 = (cand_a, cand_b), (cand2_a, cand2_b)

    def remote(src, dst, send_sem, recv_sem, where):
        copy = pltpu.make_async_remote_copy(
            src_ref=src, dst_ref=dst, send_sem=send_sem, recv_sem=recv_sem,
            device_id=where, device_id_type=MESH,
        )
        return copy

    def send(*args):
        copy = remote(*args)
        copy.start()
        sends.append(copy)

    def wait_recv(ref, recv_sem):
        remote(ref, ref, recv_sem, recv_sem, sibling).wait_recv()

    for v in range(WAVES):
        for j in range(1, PLANE):
            to = (s + j) % PLANE
            send(mine.at[v, to], cand[v].at[s], rs1_send.at[v, j], rs1_recv.at[v, s], plane_device(to))
        cand[v][s] = mine[v, s]
    send(spec_ref, spec_in, spec_send, spec_recv, partner)

    def modulate(hh, first_window, last_window):
        def body(i, carry):
            w, r = i // 8, (i % 8) * 4
            for g in range(4):
                cosine = cos_ref[:, g * LANES : (g + 1) * LANES]
                sine = sin_ref[:, g * LANES : (g + 1) * LANES]
                for k in range(4):
                    row = pl.ds(r + k, 8, stride=0)
                    a = jnp.tile(spec32[w, g, row, :], (8, 1))
                    b = jnp.tile(spec32[w, 4 + g, row, :], (8, 1))
                    first = (a * cosine - b * sine).astype(jnp.bfloat16)
                    second = (b * cosine + a * sine).astype(jnp.bfloat16)
                    at = pl.ds(pl.multiple_of((r + k) * LAGS, LAGS), LAGS)
                    mod[piece(g % 2, 2 * w, g // 2), hh, at, :] = first
                    mod[piece(g % 2, 2 * w + 1, g // 2), hh, at, :] = second
            return carry

        lax.fori_loop(8 * first_window, 8 * last_window, body, 0)

    def widen(ref):
        for g in range(8):
            spec32[:, g] = ref[:, :, g * LANES : (g + 1) * LANES].astype(jnp.float32)

    widen(spec_ref)
    modulate(half, 0, 4)

    for v in range(WAVES):
        for j in range(1, PLANE):
            frm = (s + j) % PLANE
            wait_recv(cand[v].at[frm], rs1_recv.at[v, frm])
        for b in range(4):
            at = (owners[b] // 64) * 8 + owners[b] % 8
            slots[v, b // 2, :, b % 2] = cand[v][at]
        for j in range(1, COLUMN):
            to = (t + j) % COLUMN
            send(slots.at[v, to // NZ, to % NZ], cand2[v].at[half, z], rs2_send.at[v, j], rs2_recv.at[v, t], column_device(to))
        cand2[v][half, z] = slots[v, half, z]

    wait_recv(spec_in, spec_recv)
    widen(spec_in)
    modulate(1 - half, 0, 2)

    for v in range(WAVES):
        for j in range(1, COLUMN):
            frm = (t + j) % COLUMN
            wait_recv(cand2[v].at[frm // NZ, frm % NZ], rs2_recv.at[v, frm])
        for hh in range(NH):
            for bb in range(2):
                zz = (owners[2 * half + bb] // 8) % 8
                red[v, 2 * hh + bb] = cand2[v][hh, zz, bb]
        p = piece(v, z, core)
        slot = pieces.at[p, :, q]
        if v == 1:
            for j in range(1, NZ):
                send(red.at[1], slot, agz_send.at[j], agz_recv.at[z], device(x, y, (z + j) % NZ, core, half))
        for j in range(1, NX * NY):
            to = (q + j) % (NX * NY)
            where = device(to // 4, to % 4, z, core, half)
            if v == 0:
                send(red.at[0], slot, ag1_send.at[j], ag1_recv.at[q], where)
            else:
                send(red.at[1], slot, agxy_send.at[z, j], agxy_recv.at[z, q], where)
        pieces[p, :, q] = red[v]

    def multiply(indices, start):
        def body(i, carry):
            at = pl.ds(pl.multiple_of(i * ROWS, ROWS), ROWS)
            left = jnp.concatenate([mod[p, hh, at, :] for p in indices for hh in range(NH)], axis=1)
            right = jnp.concatenate(
                [
                    pieces[p, 2 * hh : 2 * hh + 2].reshape(256, LANES)
                    for p in indices
                    for hh in range(NH)
                ],
                axis=1,
            )
            result = lax.dot_general(
                left, right, (((1,), (1,)), ((), ())), preferred_element_type=jnp.float32
            )
            if not start:
                result = result + acc[at, :]
            acc[at, :] = result
            return carry

        lax.fori_loop(0, 32 * LAGS // ROWS, body, 0)

    def forward(v, zz):
        p = piece(v, zz, core)
        send(pieces.at[p], pieces.at[p], sib_send.at[v, zz], sib_recv.at[v, zz], sibling)

    p = piece(0, z, core)
    for j in range(1, NX * NY):
        frm = (q + j) % (NX * NY)
        wait_recv(pieces.at[p, :, frm], ag1_recv.at[frm])
    send(pieces.at[p], pieces.at[p], ring_send.at[0, 0], ring_recv.at[0, 0], up)
    send(pieces.at[p], pieces.at[p], ring_send.at[0, 1], ring_recv.at[0, 1], down)
    forward(0, z)
    for d in (1, 7, 2, 6, 3, 5, 4):
        zz = (z + d) % NZ
        slot = pieces.at[piece(1, zz, core), :, q]
        wait_recv(slot, agz_recv.at[zz])
        for j in range(1, NX * NY):
            to = (q + j) % (NX * NY)
            send(slot, slot, agxy_send.at[zz, j], agxy_recv.at[zz, q], device(to // 4, to % 4, z, core, half))

    def plane_ready(zz):
        for j in range(1, NX * NY):
            frm = (q + j) % (NX * NY)
            wait_recv(pieces.at[piece(1, zz, core), :, frm], agxy_recv.at[zz, frm])
        forward(1, zz)

    modulate(1 - half, 2, 3)
    plane_ready(z)
    modulate(1 - half, 3, 4)
    multiply([piece(0, z, core), piece(1, z, core)], True)

    def sibling_ready(v, zz):
        p = piece(v, zz, 1 - core)
        wait_recv(pieces.at[p], sib_recv.at[v, zz])

    ready = [z]
    for d in range(1, 5):
        below, above = (z + NZ - d) % NZ, (z + d) % NZ
        pb, pa = piece(0, below, core), piece(0, above, core)
        if d < 4:
            wait_recv(pieces.at[pb], ring_recv.at[d - 1, 0])
            if d < 3:
                send(pieces.at[pb], pieces.at[pb], ring_send.at[d, 0], ring_recv.at[d, 0], up)
            else:
                part = pieces.at[pb, 0:2]
                send(part, part, ring_send.at[d, 0], ring_recv.at[d, 0], up)
            forward(0, below)
            wait_recv(pieces.at[pa], ring_recv.at[d - 1, 1])
            if d < 3:
                send(pieces.at[pa], pieces.at[pa], ring_send.at[d, 1], ring_recv.at[d, 1], down)
            else:
                part = pieces.at[pa, 2:4]
                send(part, part, ring_send.at[d, 1], ring_recv.at[d, 1], down)
            forward(0, above)
        else:
            wait_recv(pieces.at[pb, 0:2], ring_recv.at[d - 1, 0])
            wait_recv(pieces.at[pa, 2:4], ring_recv.at[d - 1, 1])
            forward(0, below)
        for zz in (below, above)[: 2 if d < 4 else 1]:
            plane_ready(zz)
        for zz in ready:
            for v in range(WAVES):
                sibling_ready(v, zz)
        indices = [piece(v, zz, 1 - core) for zz in ready for v in range(WAVES)]
        ready = [below, above] if d < 4 else [below]
        indices += [piece(v, zz, core) for zz in ready for v in range(WAVES)]
        multiply(indices, False)
    for zz in ready:
        for v in range(WAVES):
            sibling_ready(v, zz)
        multiply([piece(0, zz, 1 - core), piece(1, zz, 1 - core)], False)

    out_ref[...] = acc[...].astype(jnp.bfloat16)
    for copy in sends:
        copy.wait_send()


def on_device(spectra, source_pool, owners, source_rows):
    cosine, sine = phase_tables()
    vmem = pl.BlockSpec(memory_space=pltpu.VMEM)
    dma = pltpu.SemaphoreType.DMA
    b16 = jnp.bfloat16
    out = pl.pallas_call(
        kernel,
        out_shape=jax.ShapeDtypeStruct((32 * LAGS, 256), b16),
        in_specs=[pl.BlockSpec(memory_space=pltpu.SMEM), vmem, vmem, vmem, vmem, pl.BlockSpec(memory_space=pl.ANY)],
        out_specs=vmem,
        scratch_shapes=[
            pltpu.VMEM((4, 256, 1024), b16),
            pltpu.VMEM((WAVES, PLANE, 8, 16, LANES), b16),
            pltpu.VMEM((PLANE, 8, 16, LANES), b16),
            pltpu.VMEM((PLANE, 8, 16, LANES), b16),
            pltpu.VMEM((WAVES, NH, NZ, 2, 16, LANES), b16),
            pltpu.VMEM((NH, NZ, 2, 16, LANES), b16),
            pltpu.VMEM((NH, NZ, 2, 16, LANES), b16),
            pltpu.VMEM((WAVES, 4, 16, LANES), b16),
            pltpu.VMEM((WAVES * NZ * NC, 4, 8, 16, LANES), b16),
            pltpu.VMEM((4, 32, 1024), b16),
            pltpu.VMEM((4, 8, 32, LANES), jnp.float32),
            pltpu.VMEM((WAVES * NZ * NC, NH, 32 * LAGS, LANES), b16),
            pltpu.VMEM((32 * LAGS, 256), jnp.float32),
            dma((4,)),
            dma((WAVES, PLANE)),
            dma((WAVES, PLANE)),
            dma((WAVES, COLUMN)),
            dma((WAVES, COLUMN)),
            dma((8,)),
            dma((8,)),
            dma((NZ,)),
            dma((NZ,)),
            dma((NZ, 8)),
            dma((NZ, 8)),
            dma((4, 2)),
            dma((4, 2)),
            dma((WAVES, NZ)),
            dma((WAVES, NZ)),
            dma,
            dma,
        ],
        compiler_params=pltpu.CompilerParams(
            collective_id=0, has_side_effects=True, vmem_limit_bytes=62 * 2**20
        ),
    )(owners, source_rows.T, jnp.asarray(cosine), jnp.asarray(sine), spectra, source_pool)
    return out.reshape(32, LAGS, 256)


def solution(mesh):
    placed = (P("win", "chan", None), P("win", "chan", None), P(), P())
    return jax.shard_map(
        on_device, mesh=mesh, in_specs=placed, out_specs=P("chan", None, "win"), check_vma=False
    )
```

```python
import functools

import jax
import jax.numpy as jnp
import numpy as np
from jax import lax
from jax.experimental import pallas as pl
from jax.experimental.pallas import tpu as pltpu
from jax.sharding import PartitionSpec as P

LAGS = 64
BINS = 512
LANES = 128
MESH = pl.DeviceIdType.MESH
NX, NZ, NY, NC, NH = 2, 8, 4, 2, 2
PLANE = NX * NY * NC
COLUMN = NH * NZ
WAVES = 2
ROWS = 512


def phase_tables():
    freq = np.arange(BINS, dtype=np.float64)
    shift = np.arange(LAGS, dtype=np.float64) - LAGS // 2
    phase = np.pi * shift[:, None] * freq[None, :] / BINS
    scale = (2.0 * BINS) ** -0.5
    return (
        (np.cos(phase) * scale).astype(np.float32),
        (np.sin(phase) * scale).astype(np.float32),
    )


def kernel(
    owners, rows_ref, cos_ref, sin_ref, spec_ref, pool_hbm, out_ref,
    pool, mine, cand_a, cand_b, slots, cand2_a, cand2_b, red, pieces, spec_in, spec32, mod, acc,
    pool_sem, rs1_send, rs1_recv, rs2_send, rs2_recv, ag1_send, ag1_recv,
    agz_send, agz_recv, agxy_send, agxy_recv,
    ring_send, ring_recv, sib_send, sib_recv, spec_send, spec_recv,
):
    chan = lax.axis_index("chan")
    half = lax.axis_index("win")
    x, z = chan // 64, (chan // 8) % 8
    y, core = (chan // 2) % 4, chan % 2
    q = x * NY + y
    s = q * NC + core
    t = half * NZ + z

    def device(x, y, z, core, half):
        return (x * 64 + z * 8 + y * 2 + core, half)

    def plane_device(index):
        return device(index // 8, (index // 2) % 4, z, index % 2, half)

    def column_device(index):
        return device(x, y, index % NZ, core, index // NZ)

    def piece(v, zz, cc):
        return (v * NZ + zz) * NC + cc

    up = device(x, y, (z + 1) % NZ, core, half)
    down = device(x, y, (z + NZ - 1) % NZ, core, half)
    sibling = device(x, y, z, 1 - core, half)
    partner = device(x, y, z, core, 1 - half)

    loads = []
    for w in range(4):
        load = pltpu.make_async_copy(pool_hbm.at[w], pool.at[w], pool_sem.at[w])
        load.start()
        loads.append(load)

    barrier = pltpu.get_barrier_semaphore()
    for j in range(1, PLANE):
        pl.semaphore_signal(
            barrier, inc=1, device_id=plane_device((s + j) % PLANE), device_id_type=MESH
        )
    for j in range(1, COLUMN):
        pl.semaphore_signal(
            barrier, inc=1, device_id=column_device((t + j) % COLUMN), device_id_type=MESH
        )

    target = jnp.full((128, 1), -1, jnp.int32)
    for b in range(4):
        target = jnp.where(owners[b] == chan, rows_ref[:, b : b + 1], target)
    onehot = (lax.broadcasted_iota(jnp.int32, (128, 256), 1) == target).astype(jnp.float32)
    onehot = onehot.astype(jnp.bfloat16)
    for w in range(4):
        loads[w].wait()
        picked = jnp.dot(onehot, pool[w], preferred_element_type=jnp.float32)
        picked = picked.astype(jnp.bfloat16)
        for group in range(8):
            kh, cc, v = group // 4, (group // 2) % 2, group % 2
            for qq in range(8):
                mine[v, qq * NC + cc, 2 * w + kh] = picked[
                    qq * 16 : qq * 16 + 16, group * LANES : (group + 1) * LANES
                ]

    pl.semaphore_wait(barrier, PLANE + COLUMN - 2)

    sends = []
    cand, cand2 = (cand_a, cand_b), (cand2_a, cand2_b)

    def remote(src, dst, send_sem, recv_sem, where):
        copy = pltpu.make_async_remote_copy(
            src_ref=src, dst_ref=dst, send_sem=send_sem, recv_sem=recv_sem,
            device_id=where, device_id_type=MESH,
        )
        return copy

    def send(*args):
        copy = remote(*args)
        copy.start()
        sends.append(copy)

    def wait_recv(ref, recv_sem):
        remote(ref, ref, recv_sem, recv_sem, sibling).wait_recv()

    for v in range(WAVES):
        for j in range(1, PLANE):
            to = (s + j) % PLANE
            send(mine.at[v, to], cand[v].at[s], rs1_send.at[v, j], rs1_recv.at[v, s], plane_device(to))
        cand[v][s] = mine[v, s]
    send(spec_ref, spec_in, spec_send, spec_recv, partner)

    def modulate(hh, first_window, last_window):
        def body(i, carry):
            w, r = i // 8, (i % 8) * 4
            for g in range(4):
                cosine = cos_ref[:, g * LANES : (g + 1) * LANES]
                sine = sin_ref[:, g * LANES : (g + 1) * LANES]
                for k in range(4):
                    row = pl.ds(r + k, 8, stride=0)
                    a = jnp.tile(spec32[w, g, row, :], (8, 1))
                    b = jnp.tile(spec32[w, 4 + g, row, :], (8, 1))
                    first = (a * cosine - b * sine).astype(jnp.bfloat16)
                    second = (b * cosine + a * sine).astype(jnp.bfloat16)
                    at = pl.ds(pl.multiple_of((r + k) * LAGS, LAGS), LAGS)
                    mod[piece(g % 2, 2 * w, g // 2), hh, at, :] = first
                    mod[piece(g % 2, 2 * w + 1, g // 2), hh, at, :] = second
            return carry

        lax.fori_loop(8 * first_window, 8 * last_window, body, 0)

    def widen(ref):
        for g in range(8):
            spec32[:, g] = ref[:, :, g * LANES : (g + 1) * LANES].astype(jnp.float32)

    widen(spec_ref)
    modulate(half, 0, 4)

    for v in range(WAVES):
        for j in range(1, PLANE):
            frm = (s + j) % PLANE
            wait_recv(cand[v].at[frm], rs1_recv.at[v, frm])
        for b in range(4):
            at = (owners[b] // 64) * 8 + owners[b] % 8
            slots[v, b // 2, :, b % 2] = cand[v][at]
        for j in range(1, COLUMN):
            to = (t + j) % COLUMN
            send(slots.at[v, to // NZ, to % NZ], cand2[v].at[half, z], rs2_send.at[v, j], rs2_recv.at[v, t], column_device(to))
        cand2[v][half, z] = slots[v, half, z]

    wait_recv(spec_in, spec_recv)
    widen(spec_in)
    modulate(1 - half, 0, 2)

    for v in range(WAVES):
        for j in range(1, COLUMN):
            frm = (t + j) % COLUMN
            wait_recv(cand2[v].at[frm // NZ, frm % NZ], rs2_recv.at[v, frm])
        for hh in range(NH):
            for bb in range(2):
                zz = (owners[2 * half + bb] // 8) % 8
                red[v, 2 * hh + bb] = cand2[v][hh, zz, bb]
        p = piece(v, z, core)
        slot = pieces.at[p, :, q]
        if v == 1:
            for j in range(1, NZ):
                send(red.at[1], slot, agz_send.at[j], agz_recv.at[z], device(x, y, (z + j) % NZ, core, half))
        for j in range(1, NX * NY):
            to = (q + j) % (NX * NY)
            where = device(to // 4, to % 4, z, core, half)
            if v == 0:
                send(red.at[0], slot, ag1_send.at[j], ag1_recv.at[q], where)
            else:
                send(red.at[1], slot, agxy_send.at[z, j], agxy_recv.at[z, q], where)
        pieces[p, :, q] = red[v]

    def multiply(indices, start, last=False):
        def body(i, carry):
            at = pl.ds(pl.multiple_of(i * ROWS, ROWS), ROWS)
            left = jnp.concatenate([mod[p, hh, at, :] for p in indices for hh in range(NH)], axis=1)
            right = jnp.concatenate(
                [
                    pieces[p, 2 * hh : 2 * hh + 2].reshape(256, LANES)
                    for p in indices
                    for hh in range(NH)
                ],
                axis=1,
            )
            result = lax.dot_general(
                left, right, (((1,), (1,)), ((), ())), preferred_element_type=jnp.float32
            )
            if not start:
                result = result + acc[at, :]
            if last:
                out_ref[at, :] = result.astype(jnp.bfloat16)
            else:
                acc[at, :] = result
            return carry

        lax.fori_loop(0, 32 * LAGS // ROWS, body, 0)

    def forward(v, zz):
        p = piece(v, zz, core)
        send(pieces.at[p], pieces.at[p], sib_send.at[v, zz], sib_recv.at[v, zz], sibling)

    p = piece(0, z, core)
    for j in range(1, NX * NY):
        frm = (q + j) % (NX * NY)
        wait_recv(pieces.at[p, :, frm], ag1_recv.at[frm])
    send(pieces.at[p], pieces.at[p], ring_send.at[0, 0], ring_recv.at[0, 0], up)
    send(pieces.at[p], pieces.at[p], ring_send.at[0, 1], ring_recv.at[0, 1], down)
    forward(0, z)
    for d in (1, 7, 2, 6, 3, 5, 4):
        zz = (z + d) % NZ
        slot = pieces.at[piece(1, zz, core), :, q]
        wait_recv(slot, agz_recv.at[zz])
        for j in range(1, NX * NY):
            to = (q + j) % (NX * NY)
            send(slot, slot, agxy_send.at[zz, j], agxy_recv.at[zz, q], device(to // 4, to % 4, z, core, half))

    def plane_ready(zz):
        for j in range(1, NX * NY):
            frm = (q + j) % (NX * NY)
            wait_recv(pieces.at[piece(1, zz, core), :, frm], agxy_recv.at[zz, frm])
        forward(1, zz)

    modulate(1 - half, 2, 3)
    plane_ready(z)
    modulate(1 - half, 3, 4)
    multiply([piece(0, z, core), piece(1, z, core)], True)

    def sibling_ready(v, zz):
        p = piece(v, zz, 1 - core)
        wait_recv(pieces.at[p], sib_recv.at[v, zz])

    def products(ready, cc, last):
        for zz in ready:
            for v in range(WAVES):
                sibling_ready(v, zz)
        multiply([piece(v, zz, cc) for zz in ready for v in range(WAVES)], False, last)

    ready = [z]
    for d in range(1, 5):
        below, above = (z + NZ - d) % NZ, (z + d) % NZ
        pb, pa = piece(0, below, core), piece(0, above, core)
        if d < 4:
            wait_recv(pieces.at[pb], ring_recv.at[d - 1, 0])
            if d < 3:
                send(pieces.at[pb], pieces.at[pb], ring_send.at[d, 0], ring_recv.at[d, 0], up)
            else:
                part = pieces.at[pb, 0:2]
                send(part, part, ring_send.at[d, 0], ring_recv.at[d, 0], up)
            forward(0, below)
            wait_recv(pieces.at[pa], ring_recv.at[d - 1, 1])
            if d < 3:
                send(pieces.at[pa], pieces.at[pa], ring_send.at[d, 1], ring_recv.at[d, 1], down)
            else:
                part = pieces.at[pa, 2:4]
                send(part, part, ring_send.at[d, 1], ring_recv.at[d, 1], down)
            forward(0, above)
        else:
            products(ready, 1 - core, False)
            wait_recv(pieces.at[pb, 0:2], ring_recv.at[d - 1, 0])
            wait_recv(pieces.at[pa, 2:4], ring_recv.at[d - 1, 1])
            forward(0, below)
        for zz in (below, above)[: 2 if d < 4 else 1]:
            plane_ready(zz)
        if d < 4:
            for zz in ready:
                for v in range(WAVES):
                    sibling_ready(v, zz)
            indices = [piece(v, zz, 1 - core) for zz in ready for v in range(WAVES)]
            ready = [below, above]
            indices += [piece(v, zz, core) for zz in ready for v in range(WAVES)]
            multiply(indices, False)
        else:
            ready = [below]
            multiply([piece(v, below, core) for v in range(WAVES)], False)
    products(ready, 1 - core, True)

    for copy in sends:
        copy.wait_send()


def on_device(spectra, source_pool, owners, source_rows):
    cosine, sine = phase_tables()
    vmem = pl.BlockSpec(memory_space=pltpu.VMEM)
    dma = pltpu.SemaphoreType.DMA
    b16 = jnp.bfloat16
    out = pl.pallas_call(
        kernel,
        out_shape=jax.ShapeDtypeStruct((32 * LAGS, 256), b16),
        in_specs=[pl.BlockSpec(memory_space=pltpu.SMEM), vmem, vmem, vmem, vmem, pl.BlockSpec(memory_space=pl.ANY)],
        out_specs=vmem,
        scratch_shapes=[
            pltpu.VMEM((4, 256, 1024), b16),
            pltpu.VMEM((WAVES, PLANE, 8, 16, LANES), b16),
            pltpu.VMEM((PLANE, 8, 16, LANES), b16),
            pltpu.VMEM((PLANE, 8, 16, LANES), b16),
            pltpu.VMEM((WAVES, NH, NZ, 2, 16, LANES), b16),
            pltpu.VMEM((NH, NZ, 2, 16, LANES), b16),
            pltpu.VMEM((NH, NZ, 2, 16, LANES), b16),
            pltpu.VMEM((WAVES, 4, 16, LANES), b16),
            pltpu.VMEM((WAVES * NZ * NC, 4, 8, 16, LANES), b16),
            pltpu.VMEM((4, 32, 1024), b16),
            pltpu.VMEM((4, 8, 32, LANES), jnp.float32),
            pltpu.VMEM((WAVES * NZ * NC, NH, 32 * LAGS, LANES), b16),
            pltpu.VMEM((32 * LAGS, 256), jnp.float32),
            dma((4,)),
            dma((WAVES, PLANE)),
            dma((WAVES, PLANE)),
            dma((WAVES, COLUMN)),
            dma((WAVES, COLUMN)),
            dma((8,)),
            dma((8,)),
            dma((NZ,)),
            dma((NZ,)),
            dma((NZ, 8)),
            dma((NZ, 8)),
            dma((4, 2)),
            dma((4, 2)),
            dma((WAVES, NZ)),
            dma((WAVES, NZ)),
            dma,
            dma,
        ],
        compiler_params=pltpu.CompilerParams(
            collective_id=0, has_side_effects=True, vmem_limit_bytes=62 * 2**20
        ),
    )(owners, source_rows.T, jnp.asarray(cosine), jnp.asarray(sine), spectra, source_pool)
    return out.reshape(32, LAGS, 256)


def solution(mesh):
    placed = (P("win", "chan", None), P("win", "chan", None), P(), P())
    return jax.shard_map(
        on_device, mesh=mesh, in_specs=placed, out_specs=P("chan", None, "win"), check_vma=False
    )
```
